32 devices in a mesh: group: 4 (over y, core), dom: 8 (over z, x).
Axes of the slice: x: 2, y: 2, z: 4, core: 2. Of those that a mesh axis runs over, the one named last changes fastest.
Arguments:
- hidden: bfloat16 [32768, 512], P(('group', 'dom')), may hold values from -6 to 6
- enc_weight: bfloat16 [512, 512], replicated, may hold values from -0.25 to 0.25
- enc_bias: float32 [512], replicated, may hold values from -3 to 3
- enc_slope: float32 [512], replicated, may hold values from 0.05 to 0.5
- dec_token: bfloat16 [512], replicated, may hold values from -4 to 4
- dec_weight: bfloat16 [512, 128], replicated, may hold values from -0.25 to 0.25
- dec_bias: float32 [128], replicated, may hold values from -3 to 3
- targets: bfloat16 [32768, 128], P(('group', 'dom')), may hold values from -6 to 6
- local_tiles: bfloat16 [384, 128, 128], P(('group', 'dom')), may hold values from -0.375 to 0.375
- local_src: int32 [32, 12], P(('group', 'dom')), may hold values from 0 to 7
- local_dst: int32 [32, 12], P(('group', 'dom')), may hold values from 0 to 7
- local_count: int32 [32], P(('group', 'dom')), may hold values from 4 to 12, as said below
- halo_tiles: bfloat16 [256, 128, 128], P(('group', 'dom')), may hold values from -0.375 to 0.375
- halo_src: int32 [32, 8], P(('group', 'dom')), may hold values from 0 to 7, each once within a row
- halo_dst: int32 [32, 8], P(('group', 'dom')), may hold values from 0 to 7
- send_rows: int32 [256, 64], P(('group', 'dom')), may hold values from 0 to 1023
- cross_rows: int32 [128, 128], P(('group', 'dom')), may hold values from 0 to 1023
- mask_nodes: int32 [32, 512], P(('group', 'dom')), may hold values from 0 to 1023, as said below
- remask_nodes: int32 [32, 256], P(('group', 'dom')), may hold values from 0 to 1023, as said below
Outputs:
- rebuilt: bfloat16 [32768, 128], P(('group', 'dom'))
- node_error: float32 [32768], P(('group', 'dom'))
The draws below stay inside these ranges and needn't reach their ends.
Inputs may be any that keep to these rules, and one draw needn't show every extreme that they name: `local_count`: live local tiles of a partition; tile slots at or past it are ignored; some partition has 12. `halo_src`: each partition's row names each of its boundary blocks once. `mask_nodes`: distinct rows within a partition. `remask_nodes`: distinct rows within a partition.
All inputs are finite; a program needn't handle non-finite values.
Results may differ from the reference program's by a relative error of at most 0.0056.
Values may be sent and summed in bfloat16 or wider, within the bound.
No kernel may reach another device: no remote copies, remote signals or barrier semaphores. Data moves between devices by JAX's collectives and lax.ppermute only.
A program may use at most 64 MiB of HBM per device.

```python
import math
import jax
import jax.numpy as jnp
from jax import lax

D_HID = 512
D_FEAT = 128
BLK = 128
ROWS_DEV = 1024
NODES = 32768
HALO_DOM = 512
HALO_GRP = 512
HALO_BLOCKS = 8
LOCAL_TILES = 12
MASK_DEV = 512
REMASK_DEV = 256
N_GROUP = 4
N_DOM = 8


def pick_rows(key, chosen):
    device_keys = jax.random.split(key, N_GROUP * N_DOM)

    def shuffle(seed_key):
        return jax.random.permutation(seed_key, ROWS_DEV)
    orders = jax.vmap(shuffle)(device_keys)
    return orders[:, :chosen].astype(jnp.int32)


def draw_mask_nodes(key, part):
    return pick_rows(jax.random.fold_in(key, 11), MASK_DEV)


def draw_remask_nodes(key, part):
    return pick_rows(jax.random.fold_in(key, 23), REMASK_DEV)


def draw_local_count(key, part):
    devices = N_GROUP * N_DOM
    counts = jax.random.randint(jax.random.fold_in(key, 5), (devices,), LOCAL_TILES // 3, LOCAL_TILES + 1)
    spot = jax.random.randint(jax.random.fold_in(key, 7), (), 0, devices)
    return counts.at[spot].set(LOCAL_TILES).astype(jnp.int32)


def plant(result, own_key, smallest, high):
    dims = result.shape
    place = [jax.random.randint(jax.random.fold_in(own_key, axis), (), 0, dims[axis]) for axis in range(len(dims))]
    result = result.at[tuple(place)].set(smallest)
    longest = dims.index(max(dims))
    place[longest] = (place[longest] + 1) % dims[longest]
    return result.at[tuple(place)].set(high)


def shard_levels(rng, dims, cuts, low, top_value):
    factor_of = 1.0
    for dim, blocks in cuts:
        draws = jax.random.uniform(jax.random.fold_in(jax.random.fold_in(rng, 6), dim), (blocks,), jnp.float32, low / len(cuts), top_value / len(cuts))
        factor_of = factor_of * jnp.repeat(jnp.exp(draws), dims[dim] // blocks).reshape((-1,) + (1,) * (len(dims) - 1 - dim))
    return factor_of


def scatter_about(stream_key, shape, scale, bound, cuts=(), kind=jnp.bfloat16):
    level = shard_levels(stream_key, shape, cuts, -0.22, 0.18) if cuts else 1.0
    values = jax.random.normal(stream_key, shape, jnp.float32) * scale * level
    return jnp.minimum(jnp.maximum(values, -bound), bound).astype(kind)


def setup_inputs(seed: int = 0) -> dict:
    keys = jax.random.split(jax.random.key(seed), 20)
    hidden = scatter_about(keys[0], (NODES, D_HID), 1.0, 6.0, ((0, 32),))
    enc_weight = scatter_about(keys[1], (D_HID, D_HID), D_HID ** -0.5, 0.25)
    enc_bias = scatter_about(keys[2], (D_HID,), 0.5, 3.0, (), jnp.float32)
    enc_slope = jnp.clip(jnp.exp(jax.random.uniform(keys[3], (D_HID,), jnp.float32, math.log(0.05), math.log(0.5))), 0.05, 0.5)
    dec_token = scatter_about(keys[4], (D_HID,), 1.0, 4.0)
    dec_weight = scatter_about(keys[5], (D_HID, D_FEAT), D_HID ** -0.5, 0.25)
    dec_bias = scatter_about(keys[6], (D_FEAT,), 0.5, 3.0, (), jnp.float32)
    targets = scatter_about(keys[7], (NODES, D_FEAT), 1.0, 6.0, ((0, 32),))
    local_tiles = scatter_about(keys[8], (N_GROUP * N_DOM * LOCAL_TILES, BLK, BLK), (2 * BLK) ** -0.5, 0.375, ((0, 32),))
    local_src = plant(jax.random.randint(keys[9], (N_GROUP * N_DOM, LOCAL_TILES), 0, ROWS_DEV // BLK), jax.random.fold_in(keys[9], 1), 0, (ROWS_DEV // BLK) - 1).astype(jnp.int32)
    local_dst = plant(jax.random.randint(keys[10], (N_GROUP * N_DOM, LOCAL_TILES), 0, ROWS_DEV // BLK), jax.random.fold_in(keys[10], 1), 0, (ROWS_DEV // BLK) - 1).astype(jnp.int32)
    local_count = draw_local_count(jax.random.fold_in(keys[19], 71), 0)
    halo_tiles = scatter_about(keys[12], (N_GROUP * N_DOM * HALO_BLOCKS, BLK, BLK), (2 * BLK) ** -0.5, 0.375, ((0, 32),))
    halo_src = jax.vmap(lambda own: jax.random.permutation(own, HALO_BLOCKS))(jax.random.split(keys[13], (N_GROUP * N_DOM))).reshape((N_GROUP * N_DOM, HALO_BLOCKS)).astype(jnp.int32)
    halo_dst = plant(jax.random.randint(keys[14], (N_GROUP * N_DOM, HALO_BLOCKS), 0, ROWS_DEV // BLK), jax.random.fold_in(keys[14], 1), 0, (ROWS_DEV // BLK) - 1).astype(jnp.int32)
    send_rows = plant(jax.random.randint(keys[15], (N_GROUP * N_DOM * N_DOM, HALO_DOM // N_DOM), 0, ROWS_DEV), jax.random.fold_in(keys[15], 1), 0, ROWS_DEV - 1).astype(jnp.int32)
    cross_rows = plant(jax.random.randint(keys[16], (N_GROUP * N_DOM * N_GROUP, HALO_GRP // N_GROUP), 0, ROWS_DEV), jax.random.fold_in(keys[16], 1), 0, ROWS_DEV - 1).astype(jnp.int32)
    mask_nodes = draw_mask_nodes(jax.random.fold_in(keys[19], 71), 0)
    remask_nodes = draw_remask_nodes(jax.random.fold_in(keys[19], 71), 0)
    return dict(hidden=hidden, enc_weight=enc_weight, enc_bias=enc_bias, enc_slope=enc_slope, dec_token=dec_token, dec_weight=dec_weight, dec_bias=dec_bias, targets=targets, local_tiles=local_tiles, local_src=local_src, local_dst=local_dst, local_count=local_count, halo_tiles=halo_tiles, halo_src=halo_src, halo_dst=halo_dst, send_rows=send_rows, cross_rows=cross_rows, mask_nodes=mask_nodes, remask_nodes=remask_nodes)


def project(inputs, weight):
    return jnp.dot(inputs, weight, preferred_element_type=jnp.float32).astype(jnp.bfloat16)

def halo_index(send_rows, cross_rows):
    groups = N_GROUP
    domains = N_DOM
    per_dom = HALO_DOM // domains
    per_group = HALO_GRP // groups
    group_ids = jnp.arange(groups, dtype=jnp.int32)
    domain_ids = jnp.arange(domains, dtype=jnp.int32)
    row_base = (group_ids[:, None] * domains + domain_ids[None, :]) * ROWS_DEV
    sent_rows = send_rows.astype(jnp.int32).reshape(groups, domains, domains, per_dom)
    dom_index = row_base[:, :, None, None] + sent_rows
    dom_index = jnp.transpose(dom_index, (0, 2, 1, 3)).reshape(groups * domains, HALO_DOM)
    cross_list = cross_rows.astype(jnp.int32).reshape(groups, domains, groups, per_group)
    group_index = row_base[:, :, None, None] + cross_list
    group_index = jnp.transpose(group_index, (2, 1, 0, 3)).reshape(groups * domains, HALO_GRP)
    return jnp.concatenate([dom_index, group_index], axis=1).astype(jnp.int32)

def spread(tile_values, sources, targets, live_tiles, source_pool):
    picked = source_pool[sources].astype(jnp.float32)
    partial_terms = jnp.einsum('tij,tjf->tif', tile_values.astype(jnp.float32), picked, precision=lax.Precision.HIGHEST)
    blocks = ROWS_DEV // BLK
    onehot = ((targets[None, :] == jnp.arange(blocks, dtype=jnp.int32)[:, None]) & live_tiles[None, :]).astype(jnp.float32)
    summed = jnp.einsum('nt,tif->nif', onehot, partial_terms, precision=lax.Precision.HIGHEST)
    return summed.reshape(ROWS_DEV, -1)

def propagate(features, halo_rows, local_tiles, local_src, local_dst, local_count, halo_tiles, halo_src, halo_dst):
    width = features.shape[1]
    blocks = ROWS_DEV // BLK

    def one_device(device):
        own_rows = lax.dynamic_slice_in_dim(features, device * ROWS_DEV, ROWS_DEV, 0)
        remote = features[halo_rows[device]]
        source_pool = jnp.concatenate([own_rows, remote], axis=0).reshape(-1, BLK, width)
        local_values = lax.dynamic_slice_in_dim(local_tiles, device * LOCAL_TILES, LOCAL_TILES, 0)
        remote_values = lax.dynamic_slice_in_dim(halo_tiles, device * HALO_BLOCKS, HALO_BLOCKS, 0)
        live_tiles = jnp.arange(LOCAL_TILES, dtype=jnp.int32) < local_count[device]
        every_tile = jnp.ones((HALO_BLOCKS,), dtype=jnp.bool_)
        inner = spread(local_values, local_src[device], local_dst[device], live_tiles, source_pool)
        outer = spread(remote_values, halo_src[device] + blocks, halo_dst[device], every_tile, source_pool)
        return inner + outer
    devices = jnp.arange(N_GROUP * N_DOM, dtype=jnp.int32)
    return lax.map(one_device, devices).reshape(-1, width)

def reference(hidden, enc_weight, enc_bias, enc_slope, dec_token, dec_weight, dec_bias, targets, local_tiles, local_src, local_dst, local_count, halo_tiles, halo_src, halo_dst, send_rows, cross_rows, mask_nodes, remask_nodes):
    halo_rows = halo_index(send_rows, cross_rows)
    encoded = project(hidden, enc_weight)
    summed = propagate(encoded, halo_rows, local_tiles, local_src, local_dst, local_count, halo_tiles, halo_src, halo_dst) + enc_bias[None, :]
    latent = jnp.where(summed > 0, summed, enc_slope[None, :] * summed).astype(jnp.bfloat16)
    offsets = (jnp.arange(N_GROUP * N_DOM, dtype=jnp.int32) * ROWS_DEV)[:, None]
    node_total = N_GROUP * N_DOM * ROWS_DEV
    remasked = jnp.zeros((node_total,), jnp.bool_).at[(offsets + remask_nodes.astype(jnp.int32)).reshape(-1)].set(True)
    masked = jnp.zeros((node_total,), jnp.bool_).at[(offsets + mask_nodes.astype(jnp.int32)).reshape(-1)].set(True)
    decoder_in = jnp.where(remasked[:, None], dec_token[None, :], latent)
    narrowed = project(decoder_in, dec_weight)
    decoded = propagate(narrowed, halo_rows, local_tiles, local_src, local_dst, local_count, halo_tiles, halo_src, halo_dst) + dec_bias[None, :]
    rebuilt = decoded.astype(jnp.bfloat16)
    values = rebuilt.astype(jnp.float32)
    target_values = targets.astype(jnp.float32)
    cosine = lax.optimization_barrier(jnp.mean(values * target_values, axis=1)) * lax.rsqrt(lax.optimization_barrier(jnp.mean(values * values, axis=1)) + 1e-06) * lax.rsqrt(lax.optimization_barrier(jnp.mean(target_values * target_values, axis=1)) + 1e-06)
    node_error = jnp.where(masked, (1.0 - cosine) ** 2, jnp.zeros_like(cosine))
    return (rebuilt, node_error)
```

```python
import functools

import jax
import jax.numpy as jnp
from jax import lax
from jax.experimental import pallas as pl
from jax.experimental.pallas import tpu as pltpu
from jax.sharding import PartitionSpec as P

F32 = jnp.float32
BF16 = jnp.bfloat16
VMEM = pl.BlockSpec(memory_space=pltpu.VMEM)
SMEM = pl.BlockSpec(memory_space=pltpu.SMEM)


def mm(a, b):
    return jnp.dot(a, b, preferred_element_type=F32)


def column(row):
    m = row.shape[1]
    here = lax.broadcasted_iota(jnp.int32, (m, m), 0)
    there = lax.broadcasted_iota(jnp.int32, (m, m), 1)
    return jnp.sum(jnp.where(here == there, row.astype(F32), 0.0), axis=1, keepdims=True)


def as_row(col):
    m = col.shape[0]
    here = lax.broadcasted_iota(jnp.int32, (m, m), 0)
    there = lax.broadcasted_iota(jnp.int32, (m, m), 1)
    return jnp.sum(jnp.where(here == there, col, 0.0), axis=0, keepdims=True)


def one_hot(row, width):
    ids = column(row).astype(jnp.int32)
    spots = lax.broadcasted_iota(jnp.int32, (row.shape[1], width), 1)
    return jnp.where(spots == ids, 1.0, 0.0).astype(BF16)


def listed(nodes, start, rows):
    spots = lax.broadcasted_iota(jnp.int32, (rows, nodes.shape[1]), 0) + start
    return jnp.max(jnp.where(spots == nodes, 1.0, 0.0), axis=1, keepdims=True)


def peer(me, step, size):
    if size & (size - 1) == 0:
        return me ^ step
    return lax.rem(me + step, size)


def origin(me, step, size):
    if size & (size - 1) == 0:
        return me ^ step
    return lax.rem(me + size - step, size)


def pairs(step, size):
    if size & (size - 1) == 0:
        return [(j, j ^ step) for j in range(size)]
    return [(j, (j + step) % size) for j in range(size)]


def encode_kernel(n_dom, n_grp, hidden, weight, send_rows, cross_rows, me_ref, encoded, picks, *sends):
    rows = hidden.shape[0]
    encoded[...] = mm(hidden[...], weight[...]).astype(BF16)
    at = 0
    for step in range(n_dom):
        m = send_rows.shape[1]
        ids = send_rows[pl.ds(peer(me_ref[1], step, n_dom), 1), :]
        picks[at : at + m, :] = one_hot(ids, rows)
        at += m
    for step in range(n_grp):
        m = cross_rows.shape[1]
        ids = cross_rows[pl.ds(peer(me_ref[0], step, n_grp), 1), :]
        picks[at : at + m, :] = one_hot(ids, rows)
        at += m
    gather(picks, encoded, sends)


def gather(picks, source, sends):
    got = mm(picks[...], source[...]).astype(BF16)
    at = 0
    for send in sends:
        m = send.shape[0]
        send[...] = got[at : at + m, :]
        at += m


def local_kernel(blk, encoded, tiles, src, dst, count, halo_tiles, halo_src, halo_dst, bias, remask, total, halo, masked):
    rows = encoded.shape[0]
    total[...] = jnp.broadcast_to(bias[...], total.shape)

    def add_tile(t, carry):
        source = encoded[pl.ds(pl.multiple_of(src[0, t] * blk, blk), blk), :]
        spot = pl.ds(pl.multiple_of(dst[0, t] * blk, blk), blk)
        total[spot, :] += mm(tiles[t], source)
        return carry

    lax.fori_loop(0, count[0], add_tile, 0)
    halo[...] = jnp.zeros(halo.shape, BF16)
    for t in range(halo_tiles.shape[0]):
        down = pl.ds(pl.multiple_of(halo_dst[0, t] * blk, blk), blk)
        across = pl.ds(pl.multiple_of(halo_src[0, t] * blk, blk), blk)
        halo[down, across] = halo_tiles[t]
    for n in range(rows // blk):
        hit = listed(remask[...], n * blk, blk)
        masked[n * blk : (n + 1) * blk, :] = jnp.broadcast_to(hit, (blk, masked.shape[1]))


def fill_pool(n_dom, n_grp, me_ref, parts, pool):
    dom_parts, grp_parts = parts[:n_dom], parts[n_dom:]
    m = dom_parts[0].shape[0]
    for step, part in enumerate(dom_parts):
        pool[pl.ds(pl.multiple_of(origin(me_ref[1], step, n_dom) * m, m), m), :] = part[...]
    base = n_dom * m
    k = grp_parts[0].shape[0]
    for step, part in enumerate(grp_parts):
        pool[pl.ds(pl.multiple_of(base + origin(me_ref[0], step, n_grp) * k, k), k), :] = part[...]


def latent_kernel(n_dom, n_grp, me_ref, total, halo, picks, masked, slope, token, weight, *rest):
    n = n_dom + n_grp
    parts, (narrowed, *sends), pool = rest[:n], rest[n:-1], rest[-1]
    fill_pool(n_dom, n_grp, me_ref, parts, pool)
    summed = total[...] + mm(halo[...], pool[...])
    latent = jnp.where(summed > 0, summed, slope[...] * summed).astype(BF16)
    shared = jnp.broadcast_to(token[...].astype(F32), (16, token.shape[1])).astype(BF16)
    replaced = mm(shared, weight[...])[0:1, :]
    narrowed[...] = jnp.where(masked[...] > 0, replaced, mm(latent, weight[...])).astype(BF16)
    gather(picks, narrowed, sends)


def narrow_local_kernel(blk, narrowed, tiles, src, dst, count, bias, targets, nodes, total, scale, wanted):
    total[...] = jnp.broadcast_to(bias[...], total.shape)

    def add_tile(t, carry):
        source = narrowed[pl.ds(pl.multiple_of(src[0, t] * blk, blk), blk), :]
        spot = pl.ds(pl.multiple_of(dst[0, t] * blk, blk), blk)
        total[spot, :] += mm(tiles[t], source)
        return carry

    lax.fori_loop(0, count[0], add_tile, 0)
    for n in range(scale.shape[0]):
        x = targets[n * blk : (n + 1) * blk, :].astype(F32)
        power = as_row(jnp.mean(x * x, axis=1, keepdims=True))
        scale[n : n + 1, :] = lax.rsqrt(power + 1e-06)
        wanted[n : n + 1, :] = as_row(listed(nodes[...], n * blk, blk))


def final_kernel(n_dom, n_grp, blk, me_ref, total, halo, targets, scale, wanted, *rest):
    n = n_dom + n_grp
    parts, (rebuilt, error), pool = rest[:n], rest[n:-1], rest[-1]
    fill_pool(n_dom, n_grp, me_ref, parts, pool)
    rebuilt[...] = (total[...] + mm(halo[...], pool[...])).astype(BF16)
    for b in range(scale.shape[0]):
        u = rebuilt[b * blk : (b + 1) * blk, :].astype(F32)
        x = targets[b * blk : (b + 1) * blk, :].astype(F32)
        dots = as_row(jnp.mean(u * x, axis=1, keepdims=True))
        power = as_row(jnp.mean(u * u, axis=1, keepdims=True))
        cosine = dots * lax.rsqrt(power + 1e-06) * scale[b : b + 1, :]
        error[b : b + 1, :] = jnp.where(wanted[b : b + 1, :] > 0, (1.0 - cosine) ** 2, 0.0)


def call(kernel, outs, specs, args, scratch=()):
    return pl.pallas_call(
        kernel,
        out_shape=tuple(outs),
        in_specs=specs,
        out_specs=tuple(VMEM for _ in outs),
        scratch_shapes=scratch,
    )(*args)


def exchange(sends, n_dom, n_grp):
    got = [sends[0]]
    for step in range(1, n_dom):
        got.append(lax.ppermute(sends[step], "dom", pairs(step, n_dom)))
    got.append(sends[n_dom])
    for step in range(1, n_grp):
        got.append(lax.ppermute(sends[n_dom + step], "group", pairs(step, n_grp)))
    return got


def per_device(
    n_grp,
    n_dom,
    hidden,
    enc_weight,
    enc_bias,
    enc_slope,
    dec_token,
    dec_weight,
    dec_bias,
    targets,
    local_tiles,
    local_src,
    local_dst,
    local_count,
    halo_tiles,
    halo_src,
    halo_dst,
    send_rows,
    cross_rows,
    mask_nodes,
    remask_nodes,
):
    sds = jax.ShapeDtypeStruct
    rows, width = hidden.shape
    narrow = dec_weight.shape[1]
    blk = local_tiles.shape[1]
    blocks = rows // blk
    m_dom, m_grp = send_rows.shape[1], cross_rows.shape[1]
    halo_rows = n_dom * m_dom + n_grp * m_grp
    me = jnp.stack([lax.axis_index("group"), lax.axis_index("dom")]).astype(jnp.int32)

    def slots(w):
        return [sds((m_dom, w), BF16)] * n_dom + [sds((m_grp, w), BF16)] * n_grp

    encoded, picks, *sends = call(
        functools.partial(encode_kernel, n_dom, n_grp),
        [sds((rows, width), BF16), sds((halo_rows, rows), BF16)] + slots(width),
        [VMEM, VMEM, VMEM, VMEM, SMEM],
        (hidden, enc_weight, send_rows, cross_rows, me),
    )
    got = exchange(sends, n_dom, n_grp)
    total, halo, masked = call(
        functools.partial(local_kernel, blk),
        [sds((rows, width), F32), sds((rows, halo_rows), BF16), sds((rows, narrow), F32)],
        [VMEM, VMEM, SMEM, SMEM, SMEM, VMEM, SMEM, SMEM, VMEM, VMEM],
        (encoded, local_tiles, local_src, local_dst, local_count, halo_tiles, halo_src, halo_dst, enc_bias[None, :], remask_nodes),
    )
    narrowed, *sends = call(
        functools.partial(latent_kernel, n_dom, n_grp),
        [sds((rows, narrow), BF16)] + slots(narrow),
        [SMEM] + [VMEM] * (7 + n_dom + n_grp),
        (me, total, halo, picks, masked, enc_slope[None, :], dec_token[None, :], dec_weight, *got),
        [pltpu.VMEM((halo_rows, width), BF16)],
    )
    got = exchange(sends, n_dom, n_grp)
    total, scale, wanted = call(
        functools.partial(narrow_local_kernel, blk),
        [sds((rows, narrow), F32), sds((blocks, blk), F32), sds((blocks, blk), F32)],
        [VMEM, VMEM, SMEM, SMEM, SMEM, VMEM, VMEM, VMEM],
        (narrowed, local_tiles, local_src, local_dst, local_count, dec_bias[None, :], targets, mask_nodes),
    )
    rebuilt, error = call(
        functools.partial(final_kernel, n_dom, n_grp, blk),
        [sds((rows, narrow), BF16), sds((blocks, blk), F32)],
        [SMEM] + [VMEM] * (5 + n_dom + n_grp),
        (me, total, halo, targets, scale, wanted, *got),
        [pltpu.VMEM((halo_rows, narrow), BF16)],
    )
    return rebuilt, error.reshape(-1)


def solution(mesh):
    split = ("group", "dom")
    in_specs = (
        P(split, None),
        P(),
        P(),
        P(),
        P(),
        P(),
        P(),
        P(split, None),
        P(split, None, None),
        P(split, None),
        P(split, None),
        P(split),
        P(split, None, None),
        P(split, None),
        P(split, None),
        P(split, None),
        P(split, None),
        P(split, None),
        P(split, None),
    )
    out_specs = (P(split, None), P(split))
    body = functools.partial(per_device, mesh.shape["group"], mesh.shape["dom"])
    return jax.shard_map(body, mesh=mesh, in_specs=in_specs, out_specs=out_specs, check_vma=False)
```

```python
import functools

import jax
import jax.numpy as jnp
from jax import lax
from jax.experimental import pallas as pl
from jax.experimental.pallas import tpu as pltpu
from jax.sharding import PartitionSpec as P

F32 = jnp.float32
BF16 = jnp.bfloat16
VMEM = pl.BlockSpec(memory_space=pltpu.VMEM)
HBM = pl.BlockSpec(memory_space=pltpu.HBM)
GRANT = 24 << 20


class Axis:
    def __init__(self, name, size):
        self.name, self.size = name, size
        self.inner = 2 if size % 2 == 0 else 1
        self.outer = size // self.inner

    def turn(self, place, step, size, back=False):
        if size & (size - 1) == 0:
            return place ^ step
        return (place + (size - step if back else step)) % size

    def partner(self, me, step, back=False):
        outer = self.turn(me // self.inner, step // self.inner, self.outer, back)
        inner = self.turn(me % self.inner, step % self.inner, self.inner, back)
        return outer * self.inner + inner

    def permute(self, x, step):
        return lax.ppermute(x, self.name, [(j, self.partner(j, step)) for j in range(self.size)])


def mm(a, b):
    return jnp.dot(a, b, preferred_element_type=F32)


def column(row):
    m = row.shape[1]
    here = lax.broadcasted_iota(jnp.int32, (m, m), 0)
    there = lax.broadcasted_iota(jnp.int32, (m, m), 1)
    return jnp.sum(jnp.where(here == there, row.astype(F32), 0.0), axis=1, keepdims=True)


def as_row(col):
    m = col.shape[0]
    here = lax.broadcasted_iota(jnp.int32, (m, m), 0)
    there = lax.broadcasted_iota(jnp.int32, (m, m), 1)
    return jnp.sum(jnp.where(here == there, col, 0.0), axis=0, keepdims=True)


def one_hot(row, width):
    ids = column(row).astype(jnp.int32)
    spots = lax.broadcasted_iota(jnp.int32, (row.shape[1], width), 1)
    return jnp.where(spots == ids, 1.0, 0.0).astype(BF16)


def listed(nodes, start, rows):
    spots = lax.broadcasted_iota(jnp.int32, (rows, nodes.shape[1]), 0) + start
    return jnp.max(jnp.where(spots == nodes, 1.0, 0.0), axis=1, keepdims=True)


def copies(pairs, sems):
    made = [pltpu.make_async_copy(a, b, sems.at[i]) for i, (a, b) in enumerate(pairs)]
    for copy in made:
        copy.start()
    return made


def encode_kernel(axes, n_staged, chunks, *refs):
    dom, grp = axes
    hidden_h, weight_h, send_h, cross_h = refs[:4]
    staged_h = refs[4 : 4 + n_staged]
    outs = refs[4 + n_staged : -5]
    hidden, weight, send_rows, cross_rows, sems = refs[-5:]
    encoded, picks = outs[:2]
    sends, staged = outs[2 : 2 + dom.size + grp.size], outs[2 + dom.size + grp.size :]
    rows = hidden.shape[0]
    piece = rows // chunks
    spans = [pl.ds(i * piece, piece) for i in range(chunks)]
    pairs = [(send_h, send_rows), (cross_h, cross_rows), (weight_h, weight)]
    pairs += [(hidden_h.at[s], hidden.at[s]) for s in spans]
    pairs += list(zip(staged_h, staged))
    made = copies(pairs, sems)
    at = 0
    for axis, listing, copy in ((dom, send_rows, made[0]), (grp, cross_rows, made[1])):
        copy.wait()
        me = lax.axis_index(axis.name)
        m = listing.shape[1]
        for step in range(axis.size):
            ids = listing[pl.ds(axis.partner(me, step), 1), :]
            picks[at : at + m, :] = one_hot(ids, rows)
            at += m
    made[2].wait()
    for i, span in enumerate(spans):
        made[3 + i].wait()
        encoded[span, :] = mm(hidden[span, :], weight[...]).astype(BF16)
    got = mm(picks[...], encoded[...]).astype(BF16)
    at = 0
    for send in sends:
        m = send.shape[0]
        send[...] = got[at : at + m, :]
        at += m
    for copy in made[3 + chunks :]:
        copy.wait()


def add_tiles(blk, total, source, tiles, src, dst, count):
    def add_tile(t, carry):
        block = source[pl.ds(pl.multiple_of(src[0, t] * blk, blk), blk), :]
        spot = pl.ds(pl.multiple_of(dst[0, t] * blk, blk), blk)
        total[spot, :] += mm(tiles[t], block)
        return carry

    lax.fori_loop(0, count[0, 0], add_tile, 0)


def local_kernel(blk, encoded, tiles, halo_tiles, bias, remask, *refs):
    total, halo, masked = refs[5:8]
    src, dst, count, halo_src, halo_dst, sems = refs[8:]
    made = copies(list(zip(refs[:5], refs[8:13])), sems)
    total[...] = jnp.broadcast_to(bias[...], total.shape)
    halo[...] = jnp.zeros(halo.shape, BF16)
    for n in range(encoded.shape[0] // blk):
        hit = listed(remask[...], n * blk, blk)
        masked[n * blk : (n + 1) * blk, :] = jnp.broadcast_to(hit, (blk, masked.shape[1]))
    for copy in made:
        copy.wait()
    for t in range(halo_tiles.shape[0]):
        down = pl.ds(pl.multiple_of(halo_dst[0, t] * blk, blk), blk)
        across = pl.ds(pl.multiple_of(halo_src[0, t] * blk, blk), blk)
        halo[down, across] = halo_tiles[t]
    add_tiles(blk, total, encoded, tiles, src, dst, count)


def latent_kernel(axes, total, halo, picks, masked, slope, token, weight, *rest):
    dom, grp = axes
    n = dom.size + grp.size
    parts, outs, pool = rest[:n], rest[n:-1], rest[-1]
    at = 0
    for axis, got in ((dom, parts[: dom.size]), (grp, parts[dom.size :])):
        me = lax.axis_index(axis.name)
        m = got[0].shape[0]
        for step, part in enumerate(got):
            start = at + axis.partner(me, step, back=True) * m
            pool[pl.ds(pl.multiple_of(start, m), m), :] = part[...]
        at += axis.size * m
    summed = total[...] + mm(halo[...], pool[...])
    latent = jnp.where(summed > 0, summed, slope[...] * summed).astype(BF16)
    shared = jnp.broadcast_to(token[...].reshape(1, -1).astype(F32), (16, token.shape[0])).astype(BF16)
    replaced = mm(shared, weight[...])[0:1, :]
    narrowed = outs[0]
    narrowed[...] = jnp.where(masked[...] > 0, replaced, mm(latent, weight[...])).astype(BF16)
    sent = mm(picks[...], narrowed[...]).astype(BF16)
    at, out = 0, 1
    for axis, got in ((dom, parts[: dom.size]), (grp, parts[dom.size :])):
        m = got[0].shape[0]
        for outer in range(axis.outer):
            if outer == 0:
                for inner in range(axis.inner):
                    outs[out][...] = sent[at : at + m, :]
                    at, out = at + m, out + 1
            else:
                outs[out][...] = sent[at : at + axis.inner * m, :]
                at, out = at + axis.inner * m, out + 1


def narrow_local_kernel(blk, narrowed, tiles, bias, targets, nodes, *refs):
    total, scale, wanted = refs[3:6]
    src, dst, count, sems = refs[6:]
    made = copies(list(zip(refs[:3], refs[6:9])), sems)
    total[...] = jnp.broadcast_to(bias[...], total.shape)
    for n in range(scale.shape[0]):
        x = targets[n * blk : (n + 1) * blk, :].astype(F32)
        power = as_row(jnp.mean(x * x, axis=1, keepdims=True))
        scale[n : n + 1, :] = lax.rsqrt(power + 1e-06)
        wanted[n : n + 1, :] = as_row(listed(nodes[...], n * blk, blk))
    for copy in made:
        copy.wait()
    add_tiles(blk, total, narrowed, tiles, src, dst, count)


def forward_kernel(axes, *refs):
    at = 0
    outs = refs[sum(axis.outer for axis in axes) :]
    for axis, out in zip(axes, outs):
        m = refs[at].shape[0]
        out[0:m, :] = refs[at][...]
        for outer in range(1, axis.outer):
            out[outer * m : (outer + 1) * m, :] = refs[at + outer][m : 2 * m, :]
        at += axis.outer


def final_kernel(axes, blk, total, halo, targets, scale, wanted, *rest):
    rebuilt, error, pool = rest[-3:]
    at, ref = 0, 0
    for axis in axes:
        me = lax.axis_index(axis.name)
        stay, outer_got = rest[ref], rest[ref + 1 : ref + axis.outer]
        ref += axis.outer
        m = stay.shape[0]
        pieces = [(0, stay, 0)]
        pieces += [((1 + i) * axis.inner, got, 0) for i, got in enumerate(outer_got)]
        if axis.inner > 1:
            pieces += [(i * axis.inner + 1, rest[ref], i * m) for i in range(axis.outer)]
            ref += 1
        for step, got, where in pieces:
            start = at + axis.partner(me, step, back=True) * m
            pool[pl.ds(pl.multiple_of(start, m), m), :] = got[where : where + m, :]
        at += axis.size * m
    rebuilt[...] = (total[...] + mm(halo[...], pool[...])).astype(BF16)
    for b in range(scale.shape[0]):
        u = rebuilt[b * blk : (b + 1) * blk, :].astype(F32)
        x = targets[b * blk : (b + 1) * blk, :].astype(F32)
        dots = as_row(jnp.mean(u * x, axis=1, keepdims=True))
        power = as_row(jnp.mean(u * u, axis=1, keepdims=True))
        cosine = dots * lax.rsqrt(power + 1e-06) * scale[b : b + 1, :]
        error[b : b + 1, :] = jnp.where(wanted[b : b + 1, :] > 0, (1.0 - cosine) ** 2, 0.0)


def call(kernel, outs, specs, args, scratch=(), flops=10**9):
    return pl.pallas_call(
        kernel,
        out_shape=tuple(outs),
        in_specs=specs,
        out_specs=tuple(VMEM for _ in outs),
        scratch_shapes=scratch,
        compiler_params=pltpu.CompilerParams(vmem_limit_bytes=GRANT),
        cost_estimate=pl.CostEstimate(flops=flops, bytes_accessed=2**20, transcendentals=0),
    )(*args)


def per_device(
    n_grp,
    n_dom,
    hidden,
    enc_weight,
    enc_bias,
    enc_slope,
    dec_token,
    dec_weight,
    dec_bias,
    targets,
    local_tiles,
    local_src,
    local_dst,
    local_count,
    halo_tiles,
    halo_src,
    halo_dst,
    send_rows,
    cross_rows,
    mask_nodes,
    remask_nodes,
):
    sds = jax.ShapeDtypeStruct
    rows, width = hidden.shape
    narrow = dec_weight.shape[1]
    blk = local_tiles.shape[1]
    blocks = rows // blk
    m_dom, m_grp = send_rows.shape[1], cross_rows.shape[1]
    halo_rows = n_dom * m_dom + n_grp * m_grp
    dom, grp = axes = (Axis("dom", n_dom), Axis("group", n_grp))
    chunks = 4

    keep = lambda x: pltpu.with_memory_space_constraint(x, pltpu.HBM)
    to_stage = (
        local_tiles,
        halo_tiles,
        dec_weight,
        targets,
        enc_bias[None, :],
        enc_slope[None, :],
        dec_token,
        dec_bias[None, :],
        mask_nodes,
        remask_nodes,
    )
    slots = [sds((m_dom, width), BF16)] * n_dom + [sds((m_grp, width), BF16)] * n_grp
    encoded, picks, *outs = call(
        functools.partial(encode_kernel, axes, len(to_stage), chunks),
        [sds((rows, width), BF16), sds((halo_rows, rows), BF16)] + slots + [sds(x.shape, x.dtype) for x in to_stage],
        [HBM] * (4 + len(to_stage)),
        [keep(x) for x in (hidden, enc_weight, send_rows, cross_rows, *to_stage)],
        [
            pltpu.VMEM(hidden.shape, BF16),
            pltpu.VMEM(enc_weight.shape, BF16),
            pltpu.VMEM(send_rows.shape, jnp.int32),
            pltpu.VMEM(cross_rows.shape, jnp.int32),
            pltpu.SemaphoreType.DMA((3 + chunks + len(to_stage),)),
        ],
    )
    sends, staged = outs[: n_dom + n_grp], outs[n_dom + n_grp :]
    tiles, halo_edges, dec_weight, targets, enc_bias, enc_slope, dec_token, dec_bias, mask_nodes, remask_nodes = staged
    got = [sends[0]] + [dom.permute(sends[s], s) for s in range(1, n_dom)]
    got += [sends[n_dom]] + [grp.permute(sends[n_dom + s], s) for s in range(1, n_grp)]

    def smem(x):
        return pltpu.SMEM(x.shape, jnp.int32)

    edges = (keep(local_src), keep(local_dst), local_count[None, :])
    total, halo, masked = call(
        functools.partial(local_kernel, blk),
        [sds((rows, width), F32), sds((rows, halo_rows), BF16), sds((rows, narrow), F32)],
        [VMEM] * 5 + [HBM] * 5,
        (encoded, tiles, halo_edges, enc_bias, remask_nodes, *edges, keep(halo_src), keep(halo_dst)),
        [smem(x) for x in (*edges, halo_src, halo_dst)] + [pltpu.SemaphoreType.DMA((5,))],
    )
    slots = []
    for axis, m in ((dom, m_dom), (grp, m_grp)):
        slots += [sds((m, narrow), BF16)] * axis.inner
        slots += [sds((axis.inner * m, narrow), BF16)] * (axis.outer - 1)
    narrowed, *outs = call(
        functools.partial(latent_kernel, axes),
        [sds((rows, narrow), BF16)] + slots,
        [VMEM] * (7 + n_dom + n_grp),
        (total, halo, picks, masked, enc_slope, dec_token, dec_weight, *got),
        [pltpu.VMEM((halo_rows, width), BF16)],
    )
    stay, passing, outer_got = [], [], []
    for axis in axes:
        stay.append(outs[0])
        passing.append(outs[1 : axis.inner])
        rest, outs = outs[axis.inner : axis.inner + axis.outer - 1], outs[axis.inner + axis.outer - 1 :]
        outer_got.append([axis.permute(x, (i + 1) * axis.inner) for i, x in enumerate(rest)])
    total, scale, wanted = call(
        functools.partial(narrow_local_kernel, blk),
        [sds((rows, narrow), F32), sds((blocks, blk), F32), sds((blocks, blk), F32)],
        [VMEM] * 5 + [HBM] * 3,
        (narrowed, tiles, dec_bias, targets, mask_nodes, *edges),
        [smem(x) for x in edges] + [pltpu.SemaphoreType.DMA((3,))],
    )
    split = [i for i, axis in enumerate(axes) if axis.inner > 1]
    inner_got = [[], []]
    if split:
        args = [x for i in split for x in (*passing[i], *outer_got[i])]
        forward = call(
            functools.partial(forward_kernel, [axes[i] for i in split]),
            [sds((axes[i].outer * (m_dom, m_grp)[i], narrow), BF16) for i in split],
            [VMEM] * len(args),
            args,
            flops=10**7,
        )
        for i, x in zip(split, forward):
            inner_got[i] = [axes[i].permute(x, 1)]
    got = [x for i in range(2) for x in (stay[i], *outer_got[i], *inner_got[i])]
    rebuilt, error = call(
        functools.partial(final_kernel, axes, blk),
        [sds((rows, narrow), BF16), sds((blocks, blk), F32)],
        [VMEM] * (5 + len(got)),
        (total, halo, targets, scale, wanted, *got),
        [pltpu.VMEM((halo_rows, narrow), BF16)],
    )
    return rebuilt, error.reshape(-1)


def solution(mesh):
    split = ("group", "dom")
    in_specs = (
        P(split, None),
        P(),
        P(),
        P(),
        P(),
        P(),
        P(),
        P(split, None),
        P(split, None, None),
        P(split, None),
        P(split, None),
        P(split),
        P(split, None, None),
        P(split, None),
        P(split, None),
        P(split, None),
        P(split, None),
        P(split, None),
        P(split, None),
    )
    out_specs = (P(split, None), P(split))
    body = functools.partial(per_device, mesh.shape["group"], mesh.shape["dom"])
    return jax.shard_map(body, mesh=mesh, in_specs=in_specs, out_specs=out_specs, check_vma=False)
```

```python
import functools

import jax
import jax.numpy as jnp
from jax import lax
from jax.experimental import pallas as pl
from jax.experimental.pallas import tpu as pltpu
from jax.sharding import PartitionSpec as P


F32 = jnp.float32
BF16 = jnp.bfloat16
VMEM = pl.BlockSpec(memory_space=pltpu.VMEM)
HBM = pl.BlockSpec(memory_space=pltpu.HBM)
SMEM = pl.BlockSpec(memory_space=pltpu.SMEM)
GRANT = 24 << 20


class Axis:
    def __init__(self, name, size):
        self.name, self.size = name, size
        self.inner = 2 if size % 2 == 0 else 1
        self.outer = size // self.inner

    def turn(self, place, step, size, back=False):
        if size & (size - 1) == 0:
            return place ^ step
        return (place + (size - step if back else step)) % size

    def partner(self, me, step, back=False):
        outer = self.turn(me // self.inner, step // self.inner, self.outer, back)
        inner = self.turn(me % self.inner, step % self.inner, self.inner, back)
        return outer * self.inner + inner

    def permute(self, x, step):
        return lax.ppermute(x, self.name, [(j, self.partner(j, step)) for j in range(self.size)])


def mm(a, b):
    return jnp.dot(a, b, preferred_element_type=F32)


def column(row):
    m = row.shape[1]
    here = lax.broadcasted_iota(jnp.int32, (m, m), 0)
    there = lax.broadcasted_iota(jnp.int32, (m, m), 1)
    return jnp.sum(jnp.where(here == there, row.astype(F32), 0.0), axis=1, keepdims=True)


def as_row(col):
    m = col.shape[0]
    here = lax.broadcasted_iota(jnp.int32, (m, m), 0)
    there = lax.broadcasted_iota(jnp.int32, (m, m), 1)
    return jnp.sum(jnp.where(here == there, col, 0.0), axis=0, keepdims=True)


def one_hot(ids, width):
    spots = lax.broadcasted_iota(jnp.int32, (ids.shape[0], width), 1)
    return jnp.where(spots == ids, 1.0, 0.0).astype(BF16)


def listed(nodes, start, rows):
    spots = lax.broadcasted_iota(jnp.int32, (rows, nodes.shape[1]), 0) + start
    return jnp.max(jnp.where(spots == nodes, 1.0, 0.0), axis=1, keepdims=True)


def span(block, size):
    return pl.ds(pl.multiple_of(block * size, size), size)


def start_copies(pairs, sems, first=0):
    made = [pltpu.make_async_copy(a, b, sems.at[first + i]) for i, (a, b) in enumerate(pairs)]
    for copy in made:
        copy.start()
    return made


def wait_copies(made):
    for copy in made:
        copy.wait()


def slot_ids(axis, listing, steps):
    me = lax.axis_index(axis.name)
    for step in steps:
        ids = listing[pl.ds(axis.partner(me, step), 1), :]
        yield column(ids).astype(jnp.int32)


def encode_kernel(axes, n_staged, chunks, *refs):
    dom, grp = axes
    hidden_h, weight_h, send_h, cross_h = refs[:4]
    staged_h = refs[4 : 4 + n_staged]
    outs = refs[4 + n_staged : -4]
    hidden, weight, picks, sems = refs[-4:]
    encoded, send_rows, cross_rows = outs[:3]
    n = dom.size + grp.size - 2
    sends, staged = outs[3 : 3 + n], outs[3 + n :]
    rows = hidden.shape[0]
    spans = [pl.ds(i * (rows // chunks), rows // chunks) for i in range(chunks)]
    pairs = [(send_h, send_rows), (cross_h, cross_rows), (weight_h, weight)]
    pairs += [(hidden_h.at[s], hidden.at[s]) for s in spans]
    made = start_copies(pairs, sems)
    later = start_copies(list(zip(staged_h, staged)), sems, len(pairs))
    at = 0
    for axis, listing, copy in ((dom, send_rows, made[0]), (grp, cross_rows, made[1])):
        copy.wait()
        for ids in slot_ids(axis, listing, range(1, axis.size)):
            picks[at : at + ids.shape[0], :] = one_hot(ids, rows)
            at += ids.shape[0]
    made[2].wait()
    for i, s in enumerate(spans):
        made[3 + i].wait()
        encoded[s, :] = mm(hidden[s, :], weight[...]).astype(BF16)
    got = mm(picks[...], encoded[...]).astype(BF16)
    at = 0
    for send in sends:
        m = send.shape[0]
        send[...] = got[at : at + m, :]
        at += m
    wait_copies(later)


def add_tiles(total, parts, source, tiles, src, dst, count=None):
    n, blk = tiles.shape[:2]
    for t in range(n):
        tile = tiles[t]
        if count is not None:
            tile = jnp.where(t < count[0], tile, jnp.zeros_like(tile))
        parts[t] = mm(tile, source[span(src[0, t], blk), :])
    for t in range(n):
        total[span(dst[0, t], blk), :] += parts[t]


def local_kernel(axes, encoded, tiles, src_v, dst_v, bias, remask, send_rows, cross_rows, count, *refs):
    total, folded, upper, masked, *stay = refs[:-4]
    parts, src, dst, sems = refs[-4:]
    made = start_copies([(src_v, src), (dst_v, dst)], sems)
    blk = tiles.shape[1]
    rows = encoded.shape[0]
    half = folded.shape[1]
    total[...] = jnp.broadcast_to(bias[...], total.shape)
    at = 0
    for axis, listing, out in zip(axes, (send_rows, cross_rows), stay):
        for step, ids in enumerate(slot_ids(axis, listing, range(axis.size))):
            m = ids.shape[0]
            over = ids >= half
            folded[at : at + m, :] = one_hot(jnp.where(over, ids - half, ids), half)
            upper[at : at + m, :] = jnp.broadcast_to(jnp.where(over, 1.0, 0.0), (m, upper.shape[1]))
            if step == 0:
                out[...] = mm(one_hot(ids, rows), encoded[...]).astype(BF16)
            at += m
    for n in range(rows // blk):
        hit = listed(remask[...], n * blk, blk)
        masked[n * blk : (n + 1) * blk, :] = jnp.broadcast_to(hit, (blk, masked.shape[1]))
    wait_copies(made)
    add_tiles(total, parts, encoded, tiles, src, dst, count)


def latent_kernel(axes, total, tiles, src_v, dst_v, folded, upper, masked, slope, token, weight, *rest):
    dom, grp = axes
    n = dom.size + grp.size
    got, outs = rest[:n], rest[n:-6]
    summed, pool, parts, src, dst, sems = rest[-6:]
    made = start_copies([(src_v, src), (dst_v, dst)], sems)
    at = 0
    for axis, mine in ((dom, got[: dom.size]), (grp, got[dom.size :])):
        me = lax.axis_index(axis.name)
        m = mine[0].shape[0]
        for step, part in enumerate(mine):
            start = at + axis.partner(me, step, back=True) * m
            pool[pl.ds(pl.multiple_of(start, m), m), :] = part[...]
        at += axis.size * m
    summed[...] = total[...]
    shared = jnp.broadcast_to(token[...].reshape(1, -1).astype(F32), (16, token.shape[0])).astype(BF16)
    replaced = mm(shared, weight[...])[0:1, :]
    wait_copies(made)
    add_tiles(summed, parts, pool, tiles, src, dst)
    narrowed = outs[0]
    latent = jnp.maximum(summed[...], slope[...] * summed[...]).astype(BF16)
    narrowed[...] = jnp.where(masked[...] > 0, replaced, mm(latent, weight[...])).astype(BF16)
    half, narrow = folded.shape[1], narrowed.shape[1]
    both = jnp.concatenate([narrowed[:half, :], narrowed[half:, :]], axis=1)
    pair = mm(folded[...], both)
    sent = jnp.where(upper[...] > 0, pair[:, narrow:], pair[:, :narrow]).astype(BF16)
    at, out = 0, 1
    for axis, mine in ((dom, got[: dom.size]), (grp, got[dom.size :])):
        m = mine[0].shape[0]
        for size in [m] * axis.inner + [axis.inner * m] * (axis.outer - 1):
            outs[out][...] = sent[at : at + size, :]
            at, out = at + size, out + 1


def narrow_local_kernel(narrowed, tiles, src_v, dst_v, bias, count, total, parts, src, dst, sems):
    made = start_copies([(src_v, src), (dst_v, dst)], sems)
    total[...] = jnp.broadcast_to(bias[...], total.shape)
    wait_copies(made)
    add_tiles(total, parts, narrowed, tiles, src, dst, count)


def target_kernel(blk, targets, nodes, scale, wanted):
    for n in range(scale.shape[0]):
        x = targets[n * blk : (n + 1) * blk, :].astype(F32)
        power = as_row(jnp.mean(x * x, axis=1, keepdims=True))
        scale[n : n + 1, :] = lax.rsqrt(power + 1e-06)
        wanted[n : n + 1, :] = as_row(listed(nodes[...], n * blk, blk))


def forward_kernel(axes, *refs):
    at = 0
    outs = refs[sum(axis.outer for axis in axes) :]
    for axis, out in zip(axes, outs):
        m = refs[at].shape[0]
        out[0:m, :] = refs[at][...]
        for outer in range(1, axis.outer):
            out[outer * m : (outer + 1) * m, :] = refs[at + outer][m : 2 * m, :]
        at += axis.outer


def final_kernel(axes, total, tiles, src_v, dst_v, targets, scale, wanted, *rest):
    rebuilt, error, summed, pool, parts, src, dst, sems = rest[-8:]
    made = start_copies([(src_v, src), (dst_v, dst)], sems)
    blk = tiles.shape[1]
    at, ref = 0, 0
    for axis in axes:
        me = lax.axis_index(axis.name)
        stay, outer_got = rest[ref], rest[ref + 1 : ref + axis.outer]
        ref += axis.outer
        m = stay.shape[0]
        pieces = [(0, stay, 0)]
        pieces += [((1 + i) * axis.inner, got, 0) for i, got in enumerate(outer_got)]
        if axis.inner > 1:
            pieces += [(i * axis.inner + 1, rest[ref], i * m) for i in range(axis.outer)]
            ref += 1
        for step, got, where in pieces:
            start = at + axis.partner(me, step, back=True) * m
            pool[pl.ds(pl.multiple_of(start, m), m), :] = got[where : where + m, :]
        at += axis.size * m
    summed[...] = total[...]
    wait_copies(made)
    add_tiles(summed, parts, pool, tiles, src, dst)
    for b in range(scale.shape[0]):
        rounded = summed[b * blk : (b + 1) * blk, :].astype(BF16)
        rebuilt[b * blk : (b + 1) * blk, :] = rounded
        u = rounded.astype(F32)
        x = targets[b * blk : (b + 1) * blk, :].astype(F32)
        dots = as_row(jnp.mean(u * x, axis=1, keepdims=True))
        power = as_row(jnp.mean(u * u, axis=1, keepdims=True))
        cosine = dots * lax.rsqrt(power + 1e-06) * scale[b : b + 1, :]
        error[b : b + 1, :] = jnp.where(wanted[b : b + 1, :] > 0, (1.0 - cosine) ** 2, 0.0)


def call(kernel, outs, specs, args, scratch=(), flops=10**9):
    return pl.pallas_call(
        kernel,
        out_shape=tuple(outs),
        in_specs=specs,
        out_specs=tuple(VMEM for _ in outs),
        scratch_shapes=scratch,
        compiler_params=pltpu.CompilerParams(vmem_limit_bytes=GRANT),
        cost_estimate=pl.CostEstimate(flops=flops, bytes_accessed=2**20, transcendentals=0),
    )(*args)


def per_device(
    n_grp,
    n_dom,
    hidden,
    enc_weight,
    enc_bias,
    enc_slope,
    dec_token,
    dec_weight,
    dec_bias,
    targets,
    local_tiles,
    local_src,
    local_dst,
    local_count,
    halo_tiles,
    halo_src,
    halo_dst,
    send_rows,
    cross_rows,
    mask_nodes,
    remask_nodes,
):
    sds = jax.ShapeDtypeStruct
    i32 = jnp.int32
    rows, width = hidden.shape
    narrow = dec_weight.shape[1]
    n_tiles, blk = local_tiles.shape[:2]
    n_halo = halo_tiles.shape[0]
    blocks = rows // blk
    m_dom, m_grp = send_rows.shape[1], cross_rows.shape[1]
    halo_rows = n_dom * m_dom + n_grp * m_grp
    dom, grp = axes = (Axis("dom", n_dom), Axis("group", n_grp))
    chunks = 4
    to_stage = (
        local_tiles,
        local_src,
        local_dst,
        halo_tiles,
        halo_src,
        halo_dst,
        enc_bias[None, :],
        enc_slope[None, :],
        dec_token,
        dec_weight,
        dec_bias[None, :],
        targets,
        mask_nodes,
        remask_nodes,
    )

    def like(arrays):
        return [sds(x.shape, x.dtype) for x in arrays]

    def scalars(*arrays):
        return [pltpu.SMEM(x.shape, i32) for x in arrays] + [pltpu.SemaphoreType.DMA((len(arrays),))]

    fed = [pltpu.with_memory_space_constraint(x, pltpu.HBM) for x in (hidden, enc_weight, send_rows, cross_rows, *to_stage)]
    slots = [sds((m_dom, width), BF16)] * (n_dom - 1) + [sds((m_grp, width), BF16)] * (n_grp - 1)
    encoded, send_rows, cross_rows, *outs = call(
        functools.partial(encode_kernel, axes, len(to_stage), chunks),
        [sds((rows, width), BF16)] + like((send_rows, cross_rows)) + slots + like(to_stage),
        [HBM] * len(fed),
        fed,
        [
            pltpu.VMEM(hidden.shape, BF16),
            pltpu.VMEM(enc_weight.shape, BF16),
            pltpu.VMEM(((n_dom - 1) * m_dom + (n_grp - 1) * m_grp, rows), BF16),
            pltpu.SemaphoreType.DMA((3 + chunks + len(to_stage),)),
        ],
    )
    sends, staged = outs[: len(slots)], outs[len(slots) :]
    tiles, src, dst, halo_edges, halo_from, halo_to = staged[:6]
    enc_bias, enc_slope, dec_token, dec_weight, dec_bias, targets, mask_nodes, remask_nodes = staged[6:]
    dom_got = [dom.permute(sends[s - 1], s) for s in range(1, n_dom)]
    grp_got = [grp.permute(sends[n_dom + s - 2], s) for s in range(1, n_grp)]

    total, folded, upper, masked, dom_stay, grp_stay = call(
        functools.partial(local_kernel, axes),
        [
            sds((rows, width), F32),
            sds((halo_rows, rows // 2), BF16),
            sds((halo_rows, narrow), F32),
            sds((rows, narrow), F32),
            sds((m_dom, width), BF16),
            sds((m_grp, width), BF16),
        ],
        [VMEM] * 8 + [SMEM],
        (encoded, tiles, src, dst, enc_bias, remask_nodes, send_rows, cross_rows, local_count),
        [pltpu.VMEM((n_tiles, blk, width), F32)] + scalars(src, dst),
    )
    slots = []
    for axis, m in ((dom, m_dom), (grp, m_grp)):
        slots += [sds((m, narrow), BF16)] * axis.inner
        slots += [sds((axis.inner * m, narrow), BF16)] * (axis.outer - 1)
    args = (total, halo_edges, halo_from, halo_to, folded, upper, masked, enc_slope, dec_token, dec_weight)
    args += (dom_stay, *dom_got, grp_stay, *grp_got)
    narrowed, *outs = call(
        functools.partial(latent_kernel, axes),
        [sds((rows, narrow), BF16)] + slots,
        [VMEM] * len(args),
        args,
        [pltpu.VMEM((rows, width), F32), pltpu.VMEM((halo_rows, width), BF16), pltpu.VMEM((n_halo, blk, width), F32)]
        + scalars(halo_from, halo_to),
    )
    stay, passing, outer_got = [], [], []
    for axis in axes:
        stay.append(outs[0])
        passing.append(outs[1 : axis.inner])
        rest, outs = outs[axis.inner : axis.inner + axis.outer - 1], outs[axis.inner + axis.outer - 1 :]
        outer_got.append([axis.permute(x, (i + 1) * axis.inner) for i, x in enumerate(rest)])
    (total,) = call(
        narrow_local_kernel,
        [sds((rows, narrow), F32)],
        [VMEM] * 5 + [SMEM],
        (narrowed, tiles, src, dst, dec_bias, local_count),
        [pltpu.VMEM((n_tiles, blk, narrow), F32)] + scalars(src, dst),
    )
    scale, wanted = call(
        functools.partial(target_kernel, blk),
        [sds((blocks, blk), F32), sds((blocks, blk), F32)],
        [VMEM] * 2,
        (targets, mask_nodes),
    )
    split = [i for i, axis in enumerate(axes) if axis.inner > 1]
    inner_got = [[], []]
    if split:
        args = [x for i in split for x in (*passing[i], *outer_got[i])]
        forward = call(
            functools.partial(forward_kernel, [axes[i] for i in split]),
            [sds((axes[i].outer * (m_dom, m_grp)[i], narrow), BF16) for i in split],
            [VMEM] * len(args),
            args,
            flops=10**7,
        )
        for i, x in zip(split, forward):
            inner_got[i] = [axes[i].permute(x, 1)]
    got = [x for i in range(2) for x in (stay[i], *outer_got[i], *inner_got[i])]
    rebuilt, error = call(
        functools.partial(final_kernel, axes),
        [sds((rows, narrow), BF16), sds((blocks, blk), F32)],
        [VMEM] * (7 + len(got)),
        (total, halo_edges, halo_from, halo_to, targets, scale, wanted, *got),
        [pltpu.VMEM((rows, narrow), F32), pltpu.VMEM((halo_rows, narrow), BF16), pltpu.VMEM((n_halo, blk, narrow), F32)]
        + scalars(halo_from, halo_to),
    )
    return rebuilt, error.reshape(-1)


def solution(mesh):
    split = ("group", "dom")
    in_specs = (
        P(split, None),
        P(),
        P(),
        P(),
        P(),
        P(),
        P(),
        P(split, None),
        P(split, None, None),
        P(split, None),
        P(split, None),
        P(split),
        P(split, None, None),
        P(split, None),
        P(split, None),
        P(split, None),
        P(split, None),
        P(split, None),
        P(split, None),
    )
    out_specs = (P(split, None), P(split))
    sizes = mesh.shape["group"], mesh.shape["dom"]

    def body(*args):
        return per_device(*sizes, *args)

    return jax.shard_map(body, mesh=mesh, in_specs=in_specs, out_specs=out_specs, check_vma=False)
```

```python
import functools

import jax
import jax.numpy as jnp
from jax import lax
from jax.experimental import pallas as pl
from jax.experimental.pallas import tpu as pltpu
from jax.sharding import PartitionSpec as P


F32 = jnp.float32
BF16 = jnp.bfloat16
VMEM = pl.BlockSpec(memory_space=pltpu.VMEM)
HBM = pl.BlockSpec(memory_space=pltpu.HBM)
SMEM = pl.BlockSpec(memory_space=pltpu.SMEM)
GRANT = 24 << 20


class Axis:
    def __init__(self, name, size):
        self.name, self.size = name, size
        self.inner = 2 if size % 2 == 0 else 1
        self.outer = size // self.inner

    def turn(self, place, step, size, back=False):
        if size & (size - 1) == 0:
            return place ^ step
        return (place + (size - step if back else step)) % size

    def partner(self, me, step, back=False):
        outer = self.turn(me // self.inner, step // self.inner, self.outer, back)
        inner = self.turn(me % self.inner, step % self.inner, self.inner, back)
        return outer * self.inner + inner

    def permute(self, x, step):
        return lax.ppermute(x, self.name, [(j, self.partner(j, step)) for j in range(self.size)])


class Route:
    def __init__(self, axis, m, straight):
        self.axis, self.m = axis, m
        through = [s for s in range(axis.outer) if s not in straight] if axis.inner > 1 else []
        self.relayed = [s for s in through if s > 0]
        self.passing = int(0 in through)
        self.on = len(through)
        self.sends = []
        for s in range(axis.outer):
            if s in self.relayed:
                self.sends.append((s * axis.inner, axis.inner))
            else:
                first = 1 + self.passing if s == 0 else 0
                self.sends += [(s * axis.inner + t, 1) for t in range(first, axis.inner)]
        self.parts = 1 + len(self.sends) + (self.on > 0)

    def sizes(self):
        return [self.m] * (1 + self.passing) + [n * self.m for _, n in self.sends]

    def pieces(self):
        yield 0, 0, 0
        for i, (step, _) in enumerate(self.sends):
            yield step, 1 + i, 0
        for j, s in enumerate([0] * self.passing + self.relayed):
            yield s * self.axis.inner + 1, self.parts - 1, j * self.m

    def through(self):
        return [i for i, (_, n) in enumerate(self.sends) if n > 1]


def mm(a, b):
    return jnp.dot(a, b, preferred_element_type=F32)


def column(row):
    m = row.shape[1]
    here = lax.broadcasted_iota(jnp.int32, (m, m), 0)
    there = lax.broadcasted_iota(jnp.int32, (m, m), 1)
    return jnp.sum(jnp.where(here == there, row.astype(F32), 0.0), axis=1, keepdims=True)


def as_row(col):
    m = col.shape[0]
    here = lax.broadcasted_iota(jnp.int32, (m, m), 0)
    there = lax.broadcasted_iota(jnp.int32, (m, m), 1)
    return jnp.sum(jnp.where(here == there, col, 0.0), axis=0, keepdims=True)


def one_hot(ids, width):
    spots = lax.broadcasted_iota(jnp.int32, (ids.shape[0], width), 1)
    return jnp.where(spots == ids, 1.0, 0.0).astype(BF16)


def listed(nodes, start, rows):
    spots = lax.broadcasted_iota(jnp.int32, (rows, nodes.shape[1]), 0) + start
    return jnp.max(jnp.where(spots == nodes, 1.0, 0.0), axis=1, keepdims=True)


def span(block, size):
    return pl.ds(pl.multiple_of(block * size, size), size)


def start_copies(pairs, sems, first=0):
    made = [pltpu.make_async_copy(a, b, sems.at[first + i]) for i, (a, b) in enumerate(pairs)]
    for copy in made:
        copy.start()
    return made


def wait_copies(made):
    for copy in made:
        copy.wait()


def slot_ids(axis, listing, steps):
    me = lax.axis_index(axis.name)
    for step in steps:
        ids = listing[pl.ds(axis.partner(me, step), 1), :]
        yield column(ids).astype(jnp.int32)


def encode_kernel(routes, n_staged, chunks, *refs):
    hidden_h, weight_h, send_h, cross_h = refs[:4]
    staged_h = refs[4 : 4 + n_staged]
    outs = refs[4 + n_staged : -4]
    hidden, weight, picks, sems = refs[-4:]
    encoded, send_rows, cross_rows = outs[:3]
    n = sum(len(route.sizes()) - 1 for route in routes)
    sends, staged = outs[3 : 3 + n], outs[3 + n :]
    rows = hidden.shape[0]
    spans = [pl.ds(i * (rows // chunks), rows // chunks) for i in range(chunks)]
    pairs = [(send_h, send_rows), (cross_h, cross_rows), (weight_h, weight)]
    pairs += [(hidden_h.at[s], hidden.at[s]) for s in spans]
    made = start_copies(pairs, sems)
    later = start_copies(list(zip(staged_h, staged)), sems, len(pairs))
    at = 0
    for route, listing, copy in zip(routes, (send_rows, cross_rows), made):
        copy.wait()
        for ids in slot_ids(route.axis, listing, range(1, route.axis.size)):
            picks[at : at + ids.shape[0], :] = one_hot(ids, rows)
            at += ids.shape[0]
    made[2].wait()
    for i, s in enumerate(spans):
        made[3 + i].wait()
        encoded[s, :] = mm(hidden[s, :], weight[...]).astype(BF16)
    got = mm(picks[...], encoded[...]).astype(BF16)
    at = 0
    for send in sends:
        m = send.shape[0]
        send[...] = got[at : at + m, :]
        at += m
    wait_copies(later)


def add_tiles(total, parts, source, tiles, src, dst, count=None):
    n, blk = tiles.shape[:2]
    for t in range(n):
        tile = tiles[t]
        if count is not None:
            tile = jnp.where(t < count[0], tile, jnp.zeros_like(tile))
        parts[t] = mm(tile, source[span(src[0, t], blk), :])
    for t in range(n):
        total[span(dst[0, t], blk), :] += parts[t]


def local_kernel(routes, encoded, tiles, src_v, dst_v, bias, remask, send_rows, cross_rows, count, *refs):
    total, folded, upper, masked, *stay = refs[:-4]
    parts, src, dst, sems = refs[-4:]
    made = start_copies([(src_v, src), (dst_v, dst)], sems)
    blk = tiles.shape[1]
    rows = encoded.shape[0]
    half = folded.shape[1]
    total[...] = jnp.broadcast_to(bias[...], total.shape)
    at = 0
    for route, listing, out in zip(routes, (send_rows, cross_rows), stay):
        for step, ids in enumerate(slot_ids(route.axis, listing, range(route.axis.size))):
            m = ids.shape[0]
            over = ids >= half
            folded[at : at + m, :] = one_hot(jnp.where(over, ids - half, ids), half)
            upper[at : at + m, :] = jnp.broadcast_to(jnp.where(over, 1.0, 0.0), (m, upper.shape[1]))
            if step == 0:
                out[...] = mm(one_hot(ids, rows), encoded[...]).astype(BF16)
            at += m
    for n in range(rows // blk):
        hit = listed(remask[...], n * blk, blk)
        masked[n * blk : (n + 1) * blk, :] = jnp.broadcast_to(hit, (blk, masked.shape[1]))
    wait_copies(made)
    add_tiles(total, parts, encoded, tiles, src, dst, count)


def fill_pool(routes, parts, pool):
    at, first = 0, 0
    for route in routes:
        axis, m = route.axis, route.m
        me = lax.axis_index(axis.name)
        for step, part, row in route.pieces():
            start = at + axis.partner(me, step, back=True) * m
            pool[pl.ds(pl.multiple_of(start, m), m), :] = parts[first + part][row : row + m, :]
        at += axis.size * m
        first += route.parts


def latent_kernel(wide, thin, total, tiles, src_v, dst_v, folded, upper, masked, slope, token, weight, *rest):
    n = sum(route.parts for route in wide)
    got, outs, (pool, parts, src, dst, sems) = rest[:n], rest[n:-5], rest[-5:]
    summed, narrowed = outs[:2]
    made = start_copies([(src_v, src), (dst_v, dst)], sems)
    fill_pool(wide, got, pool)
    shared = jnp.broadcast_to(token[...].reshape(1, -1).astype(F32), (16, token.shape[0])).astype(BF16)
    replaced = mm(shared, weight[...])[0:1, :]
    wait_copies(made)
    add_tiles(summed, parts, pool, tiles, src, dst)
    latent = jnp.maximum(summed[...], slope[...] * summed[...]).astype(BF16)
    narrowed[...] = jnp.where(masked[...] > 0, replaced, mm(latent, weight[...])).astype(BF16)
    half, narrow = folded.shape[1], narrowed.shape[1]
    both = jnp.concatenate([narrowed[:half, :], narrowed[half:, :]], axis=1)
    pair = mm(folded[...], both)
    sent = jnp.where(upper[...] > 0, pair[:, narrow:], pair[:, :narrow]).astype(BF16)
    at = 0
    for out, size in zip(outs[2:], [size for route in thin for size in route.sizes()]):
        out[...] = sent[at : at + size, :]
        at += size


def narrow_local_kernel(narrowed, tiles, src_v, dst_v, halo_tiles, halo_src_v, halo_dst_v, bias, count, total, halo, *refs):
    parts, src, dst, halo_src, halo_dst, sems = refs
    made = start_copies([(src_v, src), (dst_v, dst), (halo_src_v, halo_src), (halo_dst_v, halo_dst)], sems)
    total[...] = jnp.broadcast_to(bias[...], total.shape)
    halo[...] = jnp.zeros(halo.shape, BF16)
    wait_copies(made)
    n, blk = halo_tiles.shape[:2]
    for t in range(n):
        halo[span(halo_dst[0, t], blk), span(halo_src[0, t], blk)] = halo_tiles[t]
    add_tiles(total, parts, narrowed, tiles, src, dst, count)


def target_kernel(blk, targets, nodes, scale, wanted):
    for n in range(scale.shape[0]):
        x = targets[n * blk : (n + 1) * blk, :].astype(F32)
        power = as_row(jnp.mean(x * x, axis=1, keepdims=True))
        scale[n : n + 1, :] = lax.rsqrt(power + 1e-06)
        wanted[n : n + 1, :] = as_row(listed(nodes[...], n * blk, blk))


def forward_kernel(routes, *refs):
    at = 0
    outs = refs[sum(route.on for route in routes) :]
    for route, out in zip(routes, outs):
        m = route.m
        for j in range(route.on):
            first = 0 if j < route.passing else m
            out[j * m : (j + 1) * m, :] = refs[at + j][first : first + m, :]
        at += route.on


def final_kernel(routes, blk, total, halo, targets, scale, wanted, *rest):
    rebuilt, error, pool = rest[-3:]
    fill_pool(routes, rest, pool)
    summed = total[...] + mm(halo[...], pool[...])
    for b in range(scale.shape[0]):
        rounded = summed[b * blk : (b + 1) * blk, :].astype(BF16)
        rebuilt[b * blk : (b + 1) * blk, :] = rounded
        u = rounded.astype(F32)
        x = targets[b * blk : (b + 1) * blk, :].astype(F32)
        dots = as_row(jnp.mean(u * x, axis=1, keepdims=True))
        power = as_row(jnp.mean(u * u, axis=1, keepdims=True))
        cosine = dots * lax.rsqrt(power + 1e-06) * scale[b : b + 1, :]
        error[b : b + 1, :] = jnp.where(wanted[b : b + 1, :] > 0, (1.0 - cosine) ** 2, 0.0)


def call(kernel, outs, specs, args, scratch=(), flops=10**9, aliases=None):
    return pl.pallas_call(
        kernel,
        out_shape=tuple(outs),
        in_specs=specs,
        out_specs=tuple(VMEM for _ in outs),
        scratch_shapes=scratch,
        input_output_aliases=aliases or {},
        compiler_params=pltpu.CompilerParams(vmem_limit_bytes=GRANT),
        cost_estimate=pl.CostEstimate(flops=flops, bytes_accessed=2**20, transcendentals=0),
    )(*args)


def send_out(routes, sends):
    passing, came = [], []
    for route in routes:
        n = route.passing
        passing.append(sends[:n])
        out, sends = sends[n : n + len(route.sends)], sends[n + len(route.sends) :]
        came.append([route.axis.permute(x, step) for x, (step, _) in zip(out, route.sends)])
    return passing, came


def send_on(routes, passing, came):
    on = [i for i, route in enumerate(routes) if route.on]
    came = [list(x) for x in came]
    if on:
        args = [x for i in on for x in (*passing[i], *(came[i][j] for j in routes[i].through()))]
        width = args[0].shape[1]
        blocks = call(
            functools.partial(forward_kernel, [routes[i] for i in on]),
            [jax.ShapeDtypeStruct((routes[i].on * routes[i].m, width), BF16) for i in on],
            [VMEM] * len(args),
            args,
            flops=10**7,
        )
        for i, x in zip(on, blocks):
            came[i].append(routes[i].axis.permute(x, 1))
    return came


def per_device(
    n_grp,
    n_dom,
    hidden,
    enc_weight,
    enc_bias,
    enc_slope,
    dec_token,
    dec_weight,
    dec_bias,
    targets,
    local_tiles,
    local_src,
    local_dst,
    local_count,
    halo_tiles,
    halo_src,
    halo_dst,
    send_rows,
    cross_rows,
    mask_nodes,
    remask_nodes,
):
    sds = jax.ShapeDtypeStruct
    i32 = jnp.int32
    rows, width = hidden.shape
    narrow = dec_weight.shape[1]
    n_tiles, blk = local_tiles.shape[:2]
    n_halo = halo_tiles.shape[0]
    blocks = rows // blk
    m_dom, m_grp = send_rows.shape[1], cross_rows.shape[1]
    halo_rows = n_dom * m_dom + n_grp * m_grp
    chunks = 4
    to_stage = (
        local_tiles,
        local_src,
        local_dst,
        halo_tiles,
        halo_src,
        halo_dst,
        enc_bias[None, :],
        enc_slope[None, :],
        dec_token,
        dec_weight,
        dec_bias[None, :],
        targets,
        mask_nodes,
        remask_nodes,
    )

    def like(arrays):
        return [sds(x.shape, x.dtype) for x in arrays]

    def scalars(*arrays):
        return [pltpu.SMEM(x.shape, i32) for x in arrays] + [pltpu.SemaphoreType.DMA((len(arrays),))]

    fed = [pltpu.with_memory_space_constraint(x, pltpu.HBM) for x in (hidden, enc_weight, send_rows, cross_rows, *to_stage)]
    wide, thin = routes(n_dom, n_grp, m_dom, m_grp)
    slots = [sds((size, width), BF16) for route in wide for size in route.sizes()[1:]]
    encoded, send_rows, cross_rows, *outs = call(
        functools.partial(encode_kernel, wide, len(to_stage), chunks),
        [sds((rows, width), BF16)] + like((send_rows, cross_rows)) + slots + like(to_stage),
        [HBM] * len(fed),
        fed,
        [
            pltpu.VMEM(hidden.shape, BF16),
            pltpu.VMEM(enc_weight.shape, BF16),
            pltpu.VMEM(((n_dom - 1) * m_dom + (n_grp - 1) * m_grp, rows), BF16),
            pltpu.SemaphoreType.DMA((3 + chunks + len(to_stage),)),
        ],
    )
    sends, staged = outs[: len(slots)], outs[len(slots) :]
    tiles, src, dst, halo_edges, halo_from, halo_to = staged[:6]
    enc_bias, enc_slope, dec_token, dec_weight, dec_bias, targets, mask_nodes, remask_nodes = staged[6:]
    passing, came = send_out(wide, sends)
    total, folded, upper, masked, *stay = call(
        functools.partial(local_kernel, wide),
        [
            sds((rows, width), F32),
            sds((halo_rows, rows // 2), BF16),
            sds((halo_rows, narrow), F32),
            sds((rows, narrow), F32),
            sds((m_dom, width), BF16),
            sds((m_grp, width), BF16),
        ],
        [VMEM] * 8 + [SMEM],
        (encoded, tiles, src, dst, enc_bias, remask_nodes, send_rows, cross_rows, local_count),
        [pltpu.VMEM((n_tiles, blk, width), F32)] + scalars(src, dst),
    )
    came = send_on(wide, passing, came)
    args = (total, halo_edges, halo_from, halo_to, folded, upper, masked, enc_slope, dec_token, dec_weight)
    args += (stay[0], *came[0], stay[1], *came[1])
    _, narrowed, *outs = call(
        functools.partial(latent_kernel, wide, thin),
        [sds((rows, width), F32), sds((rows, narrow), BF16)] + [sds((size, narrow), BF16) for route in thin for size in route.sizes()],
        [VMEM] * len(args),
        args,
        [pltpu.VMEM((halo_rows, width), BF16), pltpu.VMEM((n_halo, blk, width), F32)] + scalars(halo_from, halo_to),
        aliases={0: 0},
    )
    n = len(thin[0].sizes())
    stay, outs = [outs[0], outs[n]], outs[1:n] + outs[n + 1 :]
    passing, came = send_out(thin, outs)
    total, halo = call(
        narrow_local_kernel,
        [sds((rows, narrow), F32), sds((rows, halo_rows), BF16)],
        [VMEM] * 8 + [SMEM],
        (narrowed, tiles, src, dst, halo_edges, halo_from, halo_to, dec_bias, local_count),
        [pltpu.VMEM((n_tiles, blk, narrow), F32)] + scalars(src, dst, halo_from, halo_to),
    )
    scale, wanted = call(
        functools.partial(target_kernel, blk),
        [sds((blocks, blk), F32), sds((blocks, blk), F32)],
        [VMEM] * 2,
        (targets, mask_nodes),
    )
    came = send_on(thin, passing, came)
    got = (stay[0], *came[0], stay[1], *came[1])
    rebuilt, error = call(
        functools.partial(final_kernel, thin, blk),
        [sds((rows, narrow), BF16), sds((blocks, blk), F32)],
        [VMEM] * (5 + len(got)),
        (total, halo, targets, scale, wanted, *got),
        [pltpu.VMEM((halo_rows, narrow), BF16)],
    )
    return rebuilt, error.reshape(-1)


def routes(n_dom, n_grp, m_dom, m_grp):
    dom, grp = Axis("dom", n_dom), Axis("group", n_grp)
    wide = [Route(axis, m, range(axis.outer)) for axis, m in ((dom, m_dom), (grp, m_grp))]
    thin = [Route(axis, m, ()) for axis, m in ((dom, m_dom), (grp, m_grp))]
    return wide, thin


def solution(mesh):
    split = ("group", "dom")
    in_specs = (
        P(split, None),
        P(),
        P(),
        P(),
        P(),
        P(),
        P(),
        P(split, None),
        P(split, None, None),
        P(split, None),
        P(split, None),
        P(split),
        P(split, None, None),
        P(split, None),
        P(split, None),
        P(split, None),
        P(split, None),
        P(split, None),
        P(split, None),
    )
    out_specs = (P(split, None), P(split))
    sizes = mesh.shape["group"], mesh.shape["dom"]

    def body(*args):
        return per_device(*sizes, *args)

    return jax.shard_map(body, mesh=mesh, in_specs=in_specs, out_specs=out_specs, check_vma=False)
```

```python
import functools

import jax
import jax.numpy as jnp
from jax import lax
from jax.experimental import pallas as pl
from jax.experimental.pallas import tpu as pltpu
from jax.sharding import PartitionSpec as P


F32 = jnp.float32
BF16 = jnp.bfloat16
VMEM = pl.BlockSpec(memory_space=pltpu.VMEM)
HBM = pl.BlockSpec(memory_space=pltpu.HBM)
SMEM = pl.BlockSpec(memory_space=pltpu.SMEM)
GRANT = 24 << 20


class Axis:
    def __init__(self, name, size):
        self.name, self.size = name, size
        self.inner = 2 if size % 2 == 0 else 1
        self.outer = size // self.inner

    def turn(self, place, step, size, back=False):
        if size & (size - 1) == 0:
            return place ^ step
        return (place + (size - step if back else step)) % size

    def partner(self, me, step, back=False):
        outer = self.turn(me // self.inner, step // self.inner, self.outer, back)
        inner = self.turn(me % self.inner, step % self.inner, self.inner, back)
        return outer * self.inner + inner

    def permute(self, x, step):
        return lax.ppermute(x, self.name, [(j, self.partner(j, step)) for j in range(self.size)])


class Route:
    def __init__(self, axis, m, straight):
        self.axis, self.m = axis, m
        through = [s for s in range(axis.outer) if s not in straight] if axis.inner > 1 else []
        self.relayed = [s for s in through if s > 0]
        self.passing = int(0 in through)
        self.on = len(through)
        self.sends = []
        for s in range(axis.outer):
            if s in self.relayed:
                self.sends.append((s * axis.inner, axis.inner))
            else:
                first = 1 + self.passing if s == 0 else 0
                self.sends += [(s * axis.inner + t, 1) for t in range(first, axis.inner)]
        self.parts = 1 + len(self.sends) + (self.on > 0)

    def sizes(self):
        return [self.m] * (1 + self.passing) + [n * self.m for _, n in self.sends]

    def pieces(self):
        yield 0, 0, 0
        for i, (step, _) in enumerate(self.sends):
            yield step, 1 + i, 0
        for j, s in enumerate([0] * self.passing + self.relayed):
            yield s * self.axis.inner + 1, self.parts - 1, j * self.m

    def through(self):
        return [i for i, (_, n) in enumerate(self.sends) if n > 1]


def mm(a, b):
    return jnp.dot(a, b, preferred_element_type=F32)


def column(row):
    m = row.shape[1]
    here = lax.broadcasted_iota(jnp.int32, (m, m), 0)
    there = lax.broadcasted_iota(jnp.int32, (m, m), 1)
    return jnp.sum(jnp.where(here == there, row.astype(F32), 0.0), axis=1, keepdims=True)


def as_row(col):
    m = col.shape[0]
    here = lax.broadcasted_iota(jnp.int32, (m, m), 0)
    there = lax.broadcasted_iota(jnp.int32, (m, m), 1)
    return jnp.sum(jnp.where(here == there, col, 0.0), axis=0, keepdims=True)


def one_hot(ids, width):
    spots = lax.broadcasted_iota(jnp.int32, (ids.shape[0], width), 1)
    return jnp.where(spots == ids, 1.0, 0.0).astype(BF16)


def listed(nodes, start, rows):
    spots = lax.broadcasted_iota(jnp.int32, (rows, nodes.shape[1]), 0) + start
    return jnp.max(jnp.where(spots == nodes, 1.0, 0.0), axis=1, keepdims=True)


def span(block, size):
    return pl.ds(pl.multiple_of(block * size, size), size)


def start_copies(pairs, sems, first=0):
    made = [pltpu.make_async_copy(a, b, sems.at[first + i]) for i, (a, b) in enumerate(pairs)]
    for copy in made:
        copy.start()
    return made


def wait_copies(made):
    for copy in made:
        copy.wait()


def slot_ids(axis, listing, steps):
    me = lax.axis_index(axis.name)
    for step in steps:
        ids = listing[pl.ds(axis.partner(me, step), 1), :]
        yield column(ids).astype(jnp.int32)


def encode_kernel(routes, n_staged, chunks, *refs):
    hidden_h, weight_h, send_h, cross_h = refs[:4]
    staged_h = refs[4 : 4 + n_staged]
    outs = refs[4 + n_staged : -4]
    hidden, weight, picks, sems = refs[-4:]
    encoded, send_rows, cross_rows = outs[:3]
    n = sum(len(route.sizes()) - 1 for route in routes)
    sends, staged = outs[3 : 3 + n], outs[3 + n :]
    rows = hidden.shape[0]
    spans = [pl.ds(i * (rows // chunks), rows // chunks) for i in range(chunks)]
    pairs = [(send_h, send_rows), (cross_h, cross_rows), (weight_h, weight)]
    pairs += [(hidden_h.at[s], hidden.at[s]) for s in spans]
    made = start_copies(pairs, sems)
    later = start_copies(list(zip(staged_h, staged)), sems, len(pairs))
    at = 0
    for route, listing, copy in zip(routes, (send_rows, cross_rows), made):
        copy.wait()
        for ids in slot_ids(route.axis, listing, range(1, route.axis.size)):
            picks[at : at + ids.shape[0], :] = one_hot(ids, rows)
            at += ids.shape[0]
    made[2].wait()
    for i, s in enumerate(spans):
        made[3 + i].wait()
        encoded[s, :] = mm(hidden[s, :], weight[...]).astype(BF16)
    got = mm(picks[...], encoded[...]).astype(BF16)
    at = 0
    for send in sends:
        m = send.shape[0]
        send[...] = got[at : at + m, :]
        at += m
    wait_copies(later)


def add_tiles(total, parts, source, tiles, src, dst, count=None):
    n, blk = tiles.shape[:2]
    for t in range(n):
        tile = tiles[t]
        if count is not None:
            tile = jnp.where(t < count[0], tile, jnp.zeros_like(tile))
        parts[t] = mm(tile, source[span(src[0, t], blk), :])
    for t in range(n):
        total[span(dst[0, t], blk), :] += parts[t]


def local_kernel(routes, n_staged, encoded, tiles, src_v, dst_v, bias, remask, send_rows, cross_rows, count, *refs):
    staged_h, outs, (parts, src, dst, sems) = refs[:n_staged], refs[n_staged:-4], refs[-4:]
    total, folded, upper, masked = outs[:4]
    stay, staged = outs[4 : len(outs) - n_staged], outs[len(outs) - n_staged :]
    made = start_copies([(src_v, src), (dst_v, dst)], sems)
    later = start_copies(list(zip(staged_h, staged)), sems, len(made))
    blk = tiles.shape[1]
    rows = encoded.shape[0]
    half = folded.shape[1]
    total[...] = jnp.broadcast_to(bias[...], total.shape)
    at = 0
    for route, listing, out in zip(routes, (send_rows, cross_rows), stay):
        for step, ids in enumerate(slot_ids(route.axis, listing, range(route.axis.size))):
            m = ids.shape[0]
            over = ids >= half
            folded[at : at + m, :] = one_hot(jnp.where(over, ids - half, ids), half)
            upper[at : at + m, :] = jnp.broadcast_to(jnp.where(over, 1.0, 0.0), (m, upper.shape[1]))
            if step == 0:
                out[...] = mm(one_hot(ids, rows), encoded[...]).astype(BF16)
            at += m
    for n in range(rows // blk):
        hit = listed(remask[...], n * blk, blk)
        masked[n * blk : (n + 1) * blk, :] = jnp.broadcast_to(hit, (blk, masked.shape[1]))
    wait_copies(made)
    add_tiles(total, parts, encoded, tiles, src, dst, count)
    wait_copies(later)


def fill_pool(routes, parts, pool):
    at, first = 0, 0
    for route in routes:
        axis, m = route.axis, route.m
        me = lax.axis_index(axis.name)
        for step, part, row in route.pieces():
            start = at + axis.partner(me, step, back=True) * m
            pool[pl.ds(pl.multiple_of(start, m), m), :] = parts[first + part][row : row + m, :]
        at += axis.size * m
        first += route.parts


def latent_kernel(wide, thin, total, tiles, src_v, dst_v, folded, upper, masked, slope, token, weight, *rest):
    n = sum(route.parts for route in wide)
    got, outs, (pool, parts, src, dst, sems) = rest[:n], rest[n:-5], rest[-5:]
    summed, narrowed = outs[:2]
    made = start_copies([(src_v, src), (dst_v, dst)], sems)
    fill_pool(wide, got, pool)
    shared = jnp.broadcast_to(token[...].reshape(1, -1).astype(F32), (16, token.shape[0])).astype(BF16)
    replaced = mm(shared, weight[...])[0:1, :]
    wait_copies(made)
    add_tiles(summed, parts, pool, tiles, src, dst)
    quarter = summed.shape[0] // 4
    for i in range(4):
        s = pl.ds(i * quarter, quarter)
        latent = jnp.maximum(summed[s, :], slope[...] * summed[s, :]).astype(BF16)
        narrowed[s, :] = jnp.where(masked[s, :] > 0, replaced, mm(latent, weight[...])).astype(BF16)
    half, narrow = folded.shape[1], narrowed.shape[1]
    both = jnp.concatenate([narrowed[:half, :], narrowed[half:, :]], axis=1)
    pair = mm(folded[...], both)
    sent = jnp.where(upper[...] > 0, pair[:, narrow:], pair[:, :narrow]).astype(BF16)
    at = 0
    for out, size in zip(outs[2:], [size for route in thin for size in route.sizes()]):
        out[...] = sent[at : at + size, :]
        at += size


def narrow_local_kernel(narrowed, tiles, src_v, dst_v, halo_tiles, halo_src_v, halo_dst_v, bias, count, total, halo, *refs):
    parts, src, dst, halo_src, halo_dst, sems = refs
    made = start_copies([(src_v, src), (dst_v, dst), (halo_src_v, halo_src), (halo_dst_v, halo_dst)], sems)
    total[...] = jnp.broadcast_to(bias[...], total.shape)
    halo[...] = jnp.zeros(halo.shape, BF16)
    wait_copies(made)
    n, blk = halo_tiles.shape[:2]
    for t in range(n):
        halo[span(halo_dst[0, t], blk), span(halo_src[0, t], blk)] = halo_tiles[t]
    add_tiles(total, parts, narrowed, tiles, src, dst, count)


def target_kernel(blk, targets, nodes, scale, wanted):
    for n in range(scale.shape[0]):
        x = targets[n * blk : (n + 1) * blk, :].astype(F32)
        power = as_row(jnp.mean(x * x, axis=1, keepdims=True))
        scale[n : n + 1, :] = lax.rsqrt(power + 1e-06)
        wanted[n : n + 1, :] = as_row(listed(nodes[...], n * blk, blk))


def forward_kernel(routes, *refs):
    at = 0
    outs = refs[sum(route.on for route in routes) :]
    for route, out in zip(routes, outs):
        m = route.m
        for j in range(route.on):
            first = 0 if j < route.passing else m
            out[j * m : (j + 1) * m, :] = refs[at + j][first : first + m, :]
        at += route.on


def final_kernel(routes, blk, total, halo, targets, scale, wanted, *rest):
    rebuilt, error, pool = rest[-3:]
    fill_pool(routes, rest, pool)
    half = total.shape[0] // 2
    sums = [total[r : r + half, :] + mm(halo[r : r + half, :], pool[...]) for r in (0, half)]
    for b in range(scale.shape[0]):
        top = b * blk // half
        rounded = sums[top][b * blk - top * half : (b + 1) * blk - top * half, :].astype(BF16)
        rebuilt[b * blk : (b + 1) * blk, :] = rounded
        u = rounded.astype(F32)
        x = targets[b * blk : (b + 1) * blk, :].astype(F32)
        dots = as_row(jnp.mean(u * x, axis=1, keepdims=True))
        power = as_row(jnp.mean(u * u, axis=1, keepdims=True))
        cosine = dots * lax.rsqrt(power + 1e-06) * scale[b : b + 1, :]
        error[b : b + 1, :] = jnp.where(wanted[b : b + 1, :] > 0, (1.0 - cosine) ** 2, 0.0)


def call(kernel, outs, specs, args, scratch=(), flops=10**9, aliases=None):
    return pl.pallas_call(
        kernel,
        out_shape=tuple(outs),
        in_specs=specs,
        out_specs=tuple(VMEM for _ in outs),
        scratch_shapes=scratch,
        input_output_aliases=aliases or {},
        compiler_params=pltpu.CompilerParams(vmem_limit_bytes=GRANT),
        cost_estimate=pl.CostEstimate(flops=flops, bytes_accessed=2**20, transcendentals=0),
    )(*args)


def send_out(routes, sends):
    passing, came = [], []
    for route in routes:
        n = route.passing
        passing.append(sends[:n])
        out, sends = sends[n : n + len(route.sends)], sends[n + len(route.sends) :]
        came.append([route.axis.permute(x, step) for x, (step, _) in zip(out, route.sends)])
    return passing, came


def send_on(routes, passing, came):
    on = [i for i, route in enumerate(routes) if route.on]
    came = [list(x) for x in came]
    if on:
        args = [x for i in on for x in (*passing[i], *(came[i][j] for j in routes[i].through()))]
        width = args[0].shape[1]
        blocks = call(
            functools.partial(forward_kernel, [routes[i] for i in on]),
            [jax.ShapeDtypeStruct((routes[i].on * routes[i].m, width), BF16) for i in on],
            [VMEM] * len(args),
            args,
            flops=10**7,
        )
        for i, x in zip(on, blocks):
            came[i].append(routes[i].axis.permute(x, 1))
    return came


def per_device(
    n_grp,
    n_dom,
    hidden,
    enc_weight,
    enc_bias,
    enc_slope,
    dec_token,
    dec_weight,
    dec_bias,
    targets,
    local_tiles,
    local_src,
    local_dst,
    local_count,
    halo_tiles,
    halo_src,
    halo_dst,
    send_rows,
    cross_rows,
    mask_nodes,
    remask_nodes,
):
    sds = jax.ShapeDtypeStruct
    i32 = jnp.int32
    rows, width = hidden.shape
    narrow = dec_weight.shape[1]
    n_tiles, blk = local_tiles.shape[:2]
    n_halo = halo_tiles.shape[0]
    blocks = rows // blk
    m_dom, m_grp = send_rows.shape[1], cross_rows.shape[1]
    halo_rows = n_dom * m_dom + n_grp * m_grp
    chunks = 2
    early = (local_tiles, local_src, local_dst, enc_bias[None, :], remask_nodes)
    late = (halo_tiles, halo_src, halo_dst, enc_slope[None, :], dec_token, dec_weight)
    late += (dec_bias[None, :], targets, mask_nodes)

    def like(arrays):
        return [sds(x.shape, x.dtype) for x in arrays]

    def scalars(*arrays):
        return [pltpu.SMEM(x.shape, i32) for x in arrays] + [pltpu.SemaphoreType.DMA((len(arrays),))]

    def in_hbm(arrays):
        return [pltpu.with_memory_space_constraint(x, pltpu.HBM) for x in arrays]

    fed = in_hbm((hidden, enc_weight, send_rows, cross_rows, *early))
    wide, thin = routes(n_dom, n_grp, m_dom, m_grp)
    slots = [sds((size, width), BF16) for route in wide for size in route.sizes()[1:]]
    encoded, send_rows, cross_rows, *outs = call(
        functools.partial(encode_kernel, wide, len(early), chunks),
        [sds((rows, width), BF16)] + like((send_rows, cross_rows)) + slots + like(early),
        [HBM] * len(fed),
        fed,
        [
            pltpu.VMEM(hidden.shape, BF16),
            pltpu.VMEM(enc_weight.shape, BF16),
            pltpu.VMEM(((n_dom - 1) * m_dom + (n_grp - 1) * m_grp, rows), BF16),
            pltpu.SemaphoreType.DMA((3 + chunks + len(early),)),
        ],
    )
    sends, staged = outs[: len(slots)], outs[len(slots) :]
    tiles, src, dst, enc_bias, remask_nodes = staged
    passing, came = send_out(wide, sends)
    total, folded, upper, masked, *outs = call(
        functools.partial(local_kernel, wide, len(late)),
        [
            sds((rows, width), F32),
            sds((halo_rows, rows // 2), BF16),
            sds((halo_rows, narrow), F32),
            sds((rows, narrow), F32),
            sds((m_dom, width), BF16),
            sds((m_grp, width), BF16),
        ]
        + like(late),
        [VMEM] * 8 + [SMEM] + [HBM] * len(late),
        (encoded, tiles, src, dst, enc_bias, remask_nodes, send_rows, cross_rows, local_count, *in_hbm(late)),
        [
            pltpu.VMEM((n_tiles, blk, width), F32),
            pltpu.SMEM(src.shape, i32),
            pltpu.SMEM(dst.shape, i32),
            pltpu.SemaphoreType.DMA((2 + len(late),)),
        ],
    )
    stay, staged = outs[:2], outs[2:]
    halo_edges, halo_from, halo_to, enc_slope, dec_token, dec_weight, dec_bias, targets, mask_nodes = staged
    came = send_on(wide, passing, came)
    args = (total, halo_edges, halo_from, halo_to, folded, upper, masked, enc_slope, dec_token, dec_weight)
    args += (stay[0], *came[0], stay[1], *came[1])
    _, narrowed, *outs = call(
        functools.partial(latent_kernel, wide, thin),
        [sds((rows, width), F32), sds((rows, narrow), BF16)] + [sds((size, narrow), BF16) for route in thin for size in route.sizes()],
        [VMEM] * len(args),
        args,
        [pltpu.VMEM((halo_rows, width), BF16), pltpu.VMEM((n_halo, blk, width), F32)] + scalars(halo_from, halo_to),
        aliases={0: 0},
    )
    n = len(thin[0].sizes())
    stay, outs = [outs[0], outs[n]], outs[1:n] + outs[n + 1 :]
    passing, came = send_out(thin, outs)
    total, halo = call(
        narrow_local_kernel,
        [sds((rows, narrow), F32), sds((rows, halo_rows), BF16)],
        [VMEM] * 8 + [SMEM],
        (narrowed, tiles, src, dst, halo_edges, halo_from, halo_to, dec_bias, local_count),
        [pltpu.VMEM((n_tiles, blk, narrow), F32)] + scalars(src, dst, halo_from, halo_to),
    )
    scale, wanted = call(
        functools.partial(target_kernel, blk),
        [sds((blocks, blk), F32), sds((blocks, blk), F32)],
        [VMEM] * 2,
        (targets, mask_nodes),
    )
    came = send_on(thin, passing, came)
    got = (stay[0], *came[0], stay[1], *came[1])
    rebuilt, error = call(
        functools.partial(final_kernel, thin, blk),
        [sds((rows, narrow), BF16), sds((blocks, blk), F32)],
        [VMEM] * (5 + len(got)),
        (total, halo, targets, scale, wanted, *got),
        [pltpu.VMEM((halo_rows, narrow), BF16)],
    )
    return rebuilt, error.reshape(-1)


def routes(n_dom, n_grp, m_dom, m_grp):
    dom, grp = Axis("dom", n_dom), Axis("group", n_grp)
    wide = [Route(axis, m, range(axis.outer)) for axis, m in ((dom, m_dom), (grp, m_grp))]
    thin = [Route(axis, m, ()) for axis, m in ((dom, m_dom), (grp, m_grp))]
    return wide, thin


def solution(mesh):
    split = ("group", "dom")
    in_specs = (
        P(split, None),
        P(),
        P(),
        P(),
        P(),
        P(),
        P(),
        P(split, None),
        P(split, None, None),
        P(split, None),
        P(split, None),
        P(split),
        P(split, None, None),
        P(split, None),
        P(split, None),
        P(split, None),
        P(split, None),
        P(split, None),
        P(split, None),
    )
    out_specs = (P(split, None), P(split))
    sizes = mesh.shape["group"], mesh.shape["dom"]

    def body(*args):
        return per_device(*sizes, *args)

    return jax.shard_map(body, mesh=mesh, in_specs=in_specs, out_specs=out_specs, check_vma=False)
```
